1024 devices in a mesh: replica: 128 (over z_hi, y, x, core), expert: 8 (over z_lo).
Axes of the slice: x: 4, y: 4, z: 32 (z_hi: 4, z_lo: 8; z = z_hi * 8 + z_lo), core: 2. Of those that a mesh axis runs over, the one named last changes fastest.
Arguments:
- tokens: bfloat16 [131072, 1024], P(('replica', 'expert')), may hold values from -6 to 6
- cotangent: bfloat16 [131072, 1024], P(('replica', 'expert')), may hold values from -6 to 6
- expert_ids: int32 [131072, 8], P(('replica', 'expert')), may hold values from 0 to 63, as said below
- gate_weights: float32 [131072, 8], P(('replica', 'expert')), may hold values from 0.05 to 0.5
- gate_up: bfloat16 [8, 1024, 1024], P('expert'), may hold values from -0.1875 to 0.1875
- down_weights: bfloat16 [128, 8, 512, 1024], P('replica', 'expert'), may hold values from -6 to 6
Outputs:
- layer_out: bfloat16 [131072, 1024], P(('replica', 'expert'))
- token_grad: bfloat16 [131072, 1024], P(('replica', 'expert'))
- mixed_down: bfloat16 [128, 8, 512, 1024], P('replica', 'expert')
The draws below stay inside these ranges and needn't reach their ends.
Inputs may be any that keep to these rules, and one draw needn't show every extreme that they name: `expert_ids`: each token names 8 distinct experts. Among the 128 tokens of one device, each expert below 8 is named by at most 16 tokens; in every replica one such expert is named by exactly 16 tokens of each of its 8 devices.
All inputs are finite; a program needn't handle non-finite values.
Results may differ from the reference program's by a relative error of at most 0.0075.
Values may be sent and summed in bfloat16 or wider, within the bound.
No kernel may reach another device: no remote copies, remote signals or barrier semaphores. Data moves between devices by JAX's collectives and lax.ppermute only.
A program may use at most 32 MiB of HBM per device.

```python
import math
import jax
import jax.numpy as jnp
from jax import lax

D = 1024
FW = 512
EXPERTS = 64
TOPK = 8
CAP = 16
TOK_DEV = 128
REPLICAS = 128
TOKENS = 131072
N_REPLICA = 128
N_EXPERT = 8


def draw_expert_ids(key, part):
    blocks = TOKENS // TOK_DEV
    count_key = jax.random.fold_in(key, 11)
    order_key = jax.random.fold_in(key, 12)
    other_key = jax.random.fold_in(key, 13)
    counts = jax.random.randint(count_key, (blocks, N_EXPERT), 2, CAP // 2 + 1, dtype=jnp.int32)
    block_lane = jnp.arange(blocks, dtype=jnp.int32)
    full_expert = block_lane // N_EXPERT % N_EXPERT
    expert_lane = jnp.arange(N_EXPERT, dtype=jnp.int32)
    counts = jnp.where(expert_lane[None, :] == full_expert[:, None], CAP, counts)
    token_lane = jnp.arange(TOK_DEV, dtype=jnp.int32)
    scores = jax.random.randint(order_key, (blocks, N_EXPERT, TOK_DEV), 0, 1024, dtype=jnp.int32) * TOK_DEV + token_lane[None, None, :]
    token_rank = jnp.argsort(jnp.argsort(scores, axis=-1), axis=-1).astype(jnp.int32)
    expert_named = token_rank < counts[:, :, None]
    expert_named = jnp.transpose(expert_named, (0, 2, 1)).reshape(TOKENS, N_EXPERT)
    named_int = expert_named.astype(jnp.int32)
    window_count = jnp.sum(named_int, axis=-1)
    window_slot = jnp.cumsum(named_int, axis=-1) - 1
    slot_lane = jnp.arange(TOPK, dtype=jnp.int32)
    slot_match = expert_named[:, None, :] & (window_slot[:, None, :] == slot_lane[None, :, None])
    window_ids = jnp.sum(jnp.where(slot_match, expert_lane[None, None, :], 0), axis=-1).astype(jnp.int32)
    others = EXPERTS - N_EXPERT
    other_scores = jax.random.randint(other_key, (TOKENS, others), 0, 1024, dtype=jnp.int32) * others + jnp.arange(others, dtype=jnp.int32)[None, :]
    outside = jnp.argsort(other_scores, axis=-1)[:, :TOPK].astype(jnp.int32) + N_EXPERT
    pick_slot = jnp.clip(slot_lane[None, :] - window_count[:, None], 0, TOPK - 1)
    outside_ids = jnp.take_along_axis(outside, pick_slot, axis=1)
    return jnp.where(slot_lane[None, :] < window_count[:, None], window_ids, outside_ids).astype(jnp.int32)


def level_of(key, shape, split, least, top_value):
    level, own = 1.0, jax.random.fold_in(key, 6)
    for dim, parts in split:
        steps = jnp.exp(jax.random.uniform(jax.random.fold_in(own, dim), (parts,), jnp.float32, least / len(split), top_value / len(split)))
        level = level * jnp.repeat(steps, shape[dim] // parts).reshape([-1 if axis == dim else 1 for axis in range(len(shape))])
    return level


def scatter_about(stream_key, shape, width, bound, cuts=(), held_as=jnp.bfloat16):
    array = width * jax.random.normal(stream_key, shape, jnp.float32)
    if cuts:
        array = array * level_of(stream_key, shape, cuts, -0.22, 0.18)
    return jnp.clip(array, -bound, bound).astype(held_as)


def setup_inputs(seed: int = 0) -> dict:
    key_list = jax.random.split(jax.random.key(seed), 7)
    tokens = scatter_about(key_list[0], (TOKENS, D), 1.0, 6.0, ((0, 1024),))
    cotangent = scatter_about(key_list[1], (TOKENS, D), 1.0, 6.0, ((0, 1024),))
    expert_ids = draw_expert_ids(jax.random.fold_in(key_list[6], 71), 0)
    gate_weights = jnp.clip(jnp.exp(math.log(0.5) - 2.3025851 * jax.random.uniform(key_list[3], (TOKENS, TOPK), jnp.float32) ** level_of(key_list[3], (TOKENS, TOPK), ((0, 1024),), -0.2, 0.2)), 0.05, 0.5)
    gate_up = scatter_about(key_list[4], (N_EXPERT, D, 2 * FW), D ** -0.5, 0.1875, ((0, 8),))
    down_weights = scatter_about(key_list[5], (REPLICAS, N_EXPERT, FW, D), 1.0, 6.0, ((0, 128), (1, 8)))
    return dict(tokens=tokens, cotangent=cotangent, expert_ids=expert_ids, gate_weights=gate_weights, gate_up=gate_up, down_weights=down_weights)


step_size = 2.0
mix_share = 0.5


def silu_parts(pre):
    sigmoid_value = jax.nn.sigmoid(pre)
    return pre * sigmoid_value, sigmoid_value * (1.0 + pre * (1.0 - sigmoid_value))


def weight_step(weights, hidden, routed):
    weight_scale = weights.shape[0] ** -0.5
    weight_grad = lax.dot_general(hidden, routed, (((0,), (0,)), ((), ())), preferred_element_type=jnp.float32) * weight_scale
    return (weights.astype(jnp.float32) - step_size * weight_grad).astype(jnp.bfloat16)


def expert_pass(inputs, routed, project, weights):
    hidden_width = weights.shape[0]
    weight_scale = hidden_width ** -0.5
    projected = jnp.dot(inputs, project, preferred_element_type=jnp.float32)
    gate_pre = projected[:, :hidden_width]
    up_pre = projected[:, hidden_width:]
    activated, act_slope = silu_parts(gate_pre)
    hidden = (activated * up_pre).astype(jnp.bfloat16)
    outputs = (jnp.dot(hidden, weights, preferred_element_type=jnp.float32) * weight_scale).astype(jnp.bfloat16)
    hidden_grad = lax.dot_general(routed, weights, (((1,), (1,)), ((), ())), preferred_element_type=jnp.float32) * weight_scale
    pre_grad = jnp.concatenate([hidden_grad * up_pre * act_slope, hidden_grad * activated], axis=1).astype(jnp.bfloat16)
    input_grad = lax.dot_general(pre_grad, project, (((1,), (1,)), ((), ())), preferred_element_type=jnp.float32).astype(jnp.bfloat16)
    updated = weight_step(weights, hidden, routed)
    return outputs, input_grad, updated


def replica_pass(tokens_block, cotangent_block, ids_block, gates_block, gate_up, down_block):
    expert_lane = jnp.arange(N_EXPERT, dtype=jnp.int32)
    slot_hits = ids_block[:, :, :, None] == expert_lane[None, None, None, :]
    expert_named = jnp.any(slot_hits, axis=2)
    gate_share = jnp.sum(jnp.where(slot_hits, gates_block[:, :, :, None], 0.0), axis=2)
    token_lane = jnp.arange(TOK_DEV, dtype=jnp.int32)
    order_key = jnp.where(expert_named, token_lane[None, :, None], TOK_DEV + token_lane[None, :, None])
    slot_order = jnp.argsort(order_key, axis=1)[:, :CAP, :].astype(jnp.int32)
    counts = jnp.sum(expert_named.astype(jnp.int32), axis=1)
    is_valid = jnp.arange(CAP, dtype=jnp.int32)[None, :, None] < counts[:, None, :]
    flat_order = slot_order.reshape(N_EXPERT, CAP * N_EXPERT)
    picked_x = jnp.take_along_axis(tokens_block, flat_order[:, :, None], axis=1).reshape(N_EXPERT, CAP, N_EXPERT, D)
    picked_x = jnp.where(is_valid[..., None], picked_x, jnp.zeros_like(picked_x))
    picked_cot = jnp.take_along_axis(cotangent_block, flat_order[:, :, None], axis=1).reshape(N_EXPERT, CAP, N_EXPERT, D)
    picked_share = jnp.take_along_axis(gate_share, slot_order, axis=1) * is_valid.astype(jnp.float32)
    routed = (picked_share[..., None] * picked_cot.astype(jnp.float32)).astype(jnp.bfloat16)
    inputs_e = jnp.transpose(picked_x, (2, 0, 1, 3)).reshape(N_EXPERT, N_EXPERT * CAP, D)
    routed_e = jnp.transpose(routed, (2, 0, 1, 3)).reshape(N_EXPERT, N_EXPERT * CAP, D)
    outputs, input_grad, updated = jax.vmap(expert_pass)(inputs_e, routed_e, gate_up, down_block)
    outputs = jnp.transpose(outputs.reshape(N_EXPERT, N_EXPERT, CAP, D), (1, 2, 0, 3))
    input_grad = jnp.transpose(input_grad.reshape(N_EXPERT, N_EXPERT, CAP, D), (1, 2, 0, 3))
    source_lane = jnp.arange(N_EXPERT, dtype=jnp.int32)[:, None, None]
    contribution = picked_share[..., None] * outputs.astype(jnp.float32)
    layer_out = jnp.zeros((N_EXPERT, TOK_DEV, D), jnp.float32).at[source_lane, slot_order].add(contribution)
    grad_terms = input_grad.astype(jnp.float32) * is_valid[..., None].astype(jnp.float32)
    token_grad = jnp.zeros((N_EXPERT, TOK_DEV, D), jnp.float32).at[source_lane, slot_order].add(grad_terms)
    return layer_out.astype(jnp.bfloat16), token_grad.astype(jnp.bfloat16), updated


def reference(tokens, cotangent, expert_ids, gate_weights, gate_up, down_weights):
    block_shape = (N_REPLICA, N_EXPERT, TOK_DEV)

    def one_replica(packed):
        return replica_pass(packed[0], packed[1], packed[2], packed[3], gate_up, packed[4])

    layer_out, token_grad, updated = lax.map(one_replica, (tokens.reshape(block_shape + (D,)), cotangent.reshape(block_shape + (D,)), expert_ids.reshape(block_shape + (TOPK,)), gate_weights.reshape(block_shape + (TOPK,)), down_weights))
    previous = jnp.roll(updated, 1, axis=0)
    mixed_down = ((1.0 - mix_share) * updated.astype(jnp.float32) + mix_share * previous.astype(jnp.float32)).astype(jnp.bfloat16)
    return layer_out.reshape(TOKENS, D), token_grad.reshape(TOKENS, D), mixed_down
```

```python
import jax
import jax.numpy as jnp
from jax import lax
from jax.experimental import pallas as pl
from jax.experimental.pallas import tpu as pltpu
from jax.sharding import PartitionSpec as P

CAP = 16
PLANE = 32
EARLY_PARTS = 8
LATE_PARTS = 4


step_size = 2.0
mix_share = 0.5

f32 = jnp.float32
bf16 = jnp.bfloat16


def place(y, x, core):
    return (y * 4 + x) * 2 + core


LAST = place(3, 3, 1)
HELPERS = (
    place(3, 0, 0),
    place(0, 3, 1),
    place(0, 0, 1),
    place(3, 2, 0),
    place(2, 3, 0),
    place(0, 1, 1),
    place(1, 0, 1),
)


def times(left, right, left_dim=1, right_dim=0):
    return lax.dot_general(
        left, right, (((left_dim,), (right_dim,)), ((), ())), preferred_element_type=f32
    )


def pick_kernel(ids, gates, tokens, cotangent, sent, shares, picks):
    experts = sent.shape[0]
    count = tokens.shape[0]
    all_ids, all_gates = ids[...], gates[...]
    named_rows, share_rows = [], []
    for e in range(experts):
        hits = all_ids == e
        named_rows.append(jnp.max(hits.astype(f32), axis=0, keepdims=True))
        share_rows.append(jnp.sum(jnp.where(hits, all_gates, 0.0), axis=0, keepdims=True))
    named = jnp.concatenate(named_rows, axis=0)
    before = (
        lax.broadcasted_iota(jnp.int32, (count, count), 0)
        <= lax.broadcasted_iota(jnp.int32, (count, count), 1)
    ).astype(bf16)
    position = jnp.where(named > 0.0, times(named.astype(bf16), before), 0.0).astype(jnp.int32)
    slot = lax.broadcasted_iota(jnp.int32, (CAP, count), 0) + 1
    picked = jnp.concatenate(
        [jnp.broadcast_to(position[e : e + 1], (CAP, count)) == slot for e in range(experts)],
        axis=0,
    )
    share = jnp.concatenate(
        [jnp.broadcast_to(share_rows[e], (CAP, count)) for e in range(experts)], axis=0
    )
    share = jnp.where(picked, share, 0.0)
    shares[...] = share
    picked = picked.astype(bf16)
    picks[...] = picked
    slot_share = jnp.sum(share, axis=1, keepdims=True)
    width = tokens.shape[1]
    rows = (experts, CAP, width)
    sent[:, :CAP, :] = times(picked, tokens[...]).astype(bf16).reshape(rows)
    sent[:, CAP:, :] = (slot_share * times(picked, cotangent[...])).astype(bf16).reshape(rows)


def expert_kernel(arrived, project, weights, back, factors, *parts):
    sources = arrived.shape[0]
    width = arrived.shape[2]
    hidden_width = weights.shape[0]
    scale = hidden_width ** (-0.5)
    rows = (sources * CAP, width)
    inputs = arrived[:, :CAP, :].reshape(rows)
    routed = arrived[:, CAP:, :].reshape(rows)
    gate_pre = times(inputs, project[:, :hidden_width])
    up_pre = times(inputs, project[:, hidden_width:])
    sigmoid_value = jax.nn.sigmoid(gate_pre)
    activated = gate_pre * sigmoid_value
    hidden = (activated * up_pre).astype(bf16)
    factors[:, :hidden_width] = hidden
    factors[:, hidden_width:] = routed
    height = rows[0] // len(parts)
    for k, part in enumerate(parts):
        part[:, :hidden_width] = hidden[k * height : (k + 1) * height]
        part[:, hidden_width:] = routed[k * height : (k + 1) * height]
    block = (sources, CAP, width)
    back[:, :CAP, :] = (times(hidden, weights[...]) * scale).astype(bf16).reshape(block)
    hidden_grad = times(routed, weights[...], 1, 1) * scale
    slope = sigmoid_value * (1.0 + gate_pre * (1.0 - sigmoid_value))
    gate_grad = (hidden_grad * up_pre * slope).astype(bf16)
    up_grad = (hidden_grad * activated).astype(bf16)
    input_grad = times(gate_grad, project[:, :hidden_width], 1, 1) + times(
        up_grad, project[:, hidden_width:], 1, 1
    )
    back[:, CAP:, :] = input_grad.astype(bf16).reshape(block)


def combine_kernel(came_back, shares, picks, layer_out, token_grad):
    experts = came_back.shape[0]
    rows = (experts * CAP, came_back.shape[2])
    share = shares[...]
    upper = share.astype(bf16)
    lower = (share - upper.astype(f32)).astype(bf16)
    outputs = came_back[:, :CAP, :].reshape(rows)
    layer_out[...] = (times(upper, outputs, 0, 0) + times(lower, outputs, 0, 0)).astype(bf16)
    token_grad[...] = times(picks[...], came_back[:, CAP:, :].reshape(rows), 0, 0).astype(bf16)


def stepped(weights, factors):
    hidden_width = weights.shape[0]
    weight_grad = times(factors[:, :hidden_width], factors[:, hidden_width:], 0, 0) * (
        hidden_width ** (-0.5)
    )
    return (weights.astype(f32) - step_size * weight_grad).astype(bf16)


def step_kernel(weights, factors, updated):
    updated[...] = stepped(weights[...], factors[...])


def mix_kernel(first, updated, near_weights, near_factors, *rest):
    far_weights = rest[:EARLY_PARTS]
    far_factors = rest[EARLY_PARTS : EARLY_PARTS + LATE_PARTS]
    mixed, held_weights, held_factors = rest[EARLY_PARTS + LATE_PARTS :]

    @pl.when(first[0] == 1)
    def _():
        for held, parts in ((held_weights, far_weights), (held_factors, far_factors)):
            height = held.shape[0] // len(parts)
            for k, part in enumerate(parts):
                held[k * height : (k + 1) * height, :] = part[...]

    @pl.when(first[0] != 1)
    def _():
        held_weights[...] = near_weights[...]
        held_factors[...] = near_factors[...]

    neighbor = stepped(held_weights[...], held_factors[...])
    mixed[...] = (
        (1.0 - mix_share) * updated[...].astype(f32) + mix_share * neighbor.astype(f32)
    ).astype(bf16)


def shape(dims, dtype=bf16):
    return jax.ShapeDtypeStruct(dims, dtype)


VMEM = pl.BlockSpec(memory_space=pltpu.VMEM)


def pick(ids, gates, tokens, cotangent, experts):
    count, width = tokens.shape
    return pl.pallas_call(
        pick_kernel,
        out_shape=(
            shape((experts, 2 * CAP, width)),
            shape((experts * CAP, count), f32),
            shape((experts * CAP, count)),
        ),
        name="pick",
    )(ids, gates, tokens, cotangent)


def expert_pass(arrived, project, weights):
    rows = arrived.shape[0] * CAP
    columns = weights.shape[0] + weights.shape[1]
    return pl.pallas_call(
        expert_kernel,
        out_shape=(shape(arrived.shape), shape((rows, columns)))
        + (shape((rows // LATE_PARTS, columns)),) * LATE_PARTS,
        name="expert_pass",
    )(arrived, project, weights)


def combine(came_back, shares, picks):
    count = shares.shape[1]
    width = came_back.shape[2]
    return pl.pallas_call(
        combine_kernel,
        out_shape=(shape((count, width)), shape((count, width))),
        name="combine",
    )(came_back, shares, picks)


def step(weights, factors):
    return pl.pallas_call(step_kernel, out_shape=shape(weights.shape), name="step")(
        weights, factors
    )


def mix(first, updated, near_weights, far_weights, near_factors, far_factors):
    whole = [VMEM] * (3 + len(far_weights) + len(far_factors))
    return pl.pallas_call(
        mix_kernel,
        out_shape=shape(updated.shape),
        in_specs=[pl.BlockSpec(memory_space=pltpu.SMEM)] + whole,
        out_specs=VMEM,
        scratch_shapes=[
            pltpu.VMEM(near_weights.shape, bf16),
            pltpu.VMEM(near_factors.shape, bf16),
        ],
        name="mix",
    )(first, updated, near_weights, near_factors, *far_weights, *far_factors)


def from_previous(array, pieces):
    replicas = lax.axis_size("replica")
    planes = [h * PLANE for h in range(replicas // PLANE)]
    held = [pieces[0]]
    for k, piece in enumerate(pieces[1:]):
        route = [(h + LAST, h + HELPERS[k]) for h in planes]
        held.append(lax.ppermute(piece, "replica", route))
    route = [(h + i, h + i + 1) for h in planes for i in range(PLANE - 1)]
    near = lax.ppermute(array, "replica", route)
    far = []
    for source, piece in zip((LAST,) + HELPERS, held):
        route = [(h + source, (h + PLANE) % replicas) for h in planes]
        far.append(lax.ppermute(piece, "replica", route))
    return near, far


def on_device(tokens, cotangent, expert_ids, gate_weights, gate_up, down_weights):
    experts = lax.axis_size("expert")
    weights = down_weights[0, 0]
    project = gate_up[0]
    sent, shares, picks = pick(expert_ids.T, gate_weights.T, tokens, cotangent, experts)
    arrived = lax.all_to_all(sent, "expert", split_axis=0, concat_axis=0, tiled=True)
    height = weights.shape[0] // EARLY_PARTS
    pieces = [weights[k * height : (k + 1) * height] for k in range(EARLY_PARTS)]
    near_weights, far_weights = from_previous(weights, pieces)
    back, factors, *parts = expert_pass(arrived, project, weights)
    came_back = lax.all_to_all(back, "expert", split_axis=0, concat_axis=0, tiled=True)
    near_factors, far_factors = from_previous(factors, parts)
    updated = step(weights, factors)
    first = (lax.axis_index("replica") % PLANE == 0).astype(jnp.int32).reshape(1)
    mixed = mix(first, updated, near_weights, far_weights, near_factors, far_factors)
    layer_out, token_grad = combine(came_back, shares, picks)
    return (layer_out, token_grad, mixed[None, None])


def solution(mesh):
    return jax.shard_map(
        on_device,
        mesh=mesh,
        in_specs=(
            P(("replica", "expert"), None),
            P(("replica", "expert"), None),
            P(("replica", "expert"), None),
            P(("replica", "expert"), None),
            P("expert", None, None),
            P("replica", "expert", None, None),
        ),
        out_specs=(
            P(("replica", "expert"), None),
            P(("replica", "expert"), None),
            P("replica", "expert", None, None),
        ),
        check_vma=False,
    )
```

```python
import jax
import jax.numpy as jnp
from jax import lax
from jax.experimental import pallas as pl
from jax.experimental.pallas import tpu as pltpu
from jax.sharding import PartitionSpec as P

CAP = 16
PLANE = 32


step_size = 2.0
mix_share = 0.5

f32 = jnp.float32
bf16 = jnp.bfloat16


def place(y, x, core):
    return (y * 4 + x) * 2 + core


LAST = place(3, 3, 1)
EARLY_FROM = (place(3, 2, 0), place(2, 3, 0), place(2, 1, 0), place(1, 2, 0))
LATE_FROM = (LAST, place(3, 0, 0), place(0, 3, 1), place(0, 0, 1))
EARLY_PARTS = len(EARLY_FROM)
LATE_PARTS = len(LATE_FROM)


def times(left, right, left_dim=1, right_dim=0):
    return lax.dot_general(
        left, right, (((left_dim,), (right_dim,)), ((), ())), preferred_element_type=f32
    )


def pick_kernel(ids_in, gates_in, tokens_in, cotangent_in, sent_out, shares_out, picks_out, *own):
    ids, gates, tokens, cotangent, sent, shares, picks, sems = own
    loads = [
        pltpu.make_async_copy(source, target, sems.at[k])
        for k, (source, target) in enumerate(
            ((ids_in, ids), (gates_in, gates), (tokens_in, tokens), (cotangent_in, cotangent))
        )
    ]
    for load in loads:
        load.start()
    experts = sent.shape[0]
    count, width = tokens.shape
    loads[0].wait()
    loads[1].wait()
    all_ids, all_gates = ids[...], gates[...]
    named_rows, share_rows = [], []
    for e in range(experts):
        hits = all_ids == e
        named_rows.append(jnp.max(hits.astype(f32), axis=0, keepdims=True))
        share_rows.append(jnp.sum(jnp.where(hits, all_gates, 0.0), axis=0, keepdims=True))
    named = jnp.concatenate(named_rows, axis=0)
    before = (
        lax.broadcasted_iota(jnp.int32, (count, count), 0)
        <= lax.broadcasted_iota(jnp.int32, (count, count), 1)
    ).astype(bf16)
    position = jnp.where(named > 0.0, times(named.astype(bf16), before), 0.0).astype(jnp.int32)
    slot = lax.broadcasted_iota(jnp.int32, (CAP, count), 0) + 1
    picked = jnp.concatenate(
        [jnp.broadcast_to(position[e : e + 1], (CAP, count)) == slot for e in range(experts)],
        axis=0,
    )
    share = jnp.concatenate(
        [jnp.broadcast_to(share_rows[e], (CAP, count)) for e in range(experts)], axis=0
    )
    share = jnp.where(picked, share, 0.0)
    shares[...] = share
    picked = picked.astype(bf16)
    picks[...] = picked
    rows = (experts, CAP, width)
    first, second = slice(0, CAP), slice(CAP, 2 * CAP)
    stores = [
        pltpu.make_async_copy(shares, shares_out, sems.at[4]),
        pltpu.make_async_copy(picks, picks_out, sems.at[5]),
        pltpu.make_async_copy(sent.at[:, first], sent_out.at[:, first], sems.at[6]),
        pltpu.make_async_copy(sent.at[:, second], sent_out.at[:, second], sems.at[7]),
    ]
    stores[0].start()
    stores[1].start()
    loads[2].wait()
    sent[:, first, :] = times(picked, tokens[...]).astype(bf16).reshape(rows)
    stores[2].start()
    slot_share = jnp.sum(share, axis=1, keepdims=True)
    loads[3].wait()
    sent[:, second, :] = (slot_share * times(picked, cotangent[...])).astype(bf16).reshape(rows)
    stores[3].start()
    for store in stores:
        store.wait()


def expert_kernel(arrived_in, project, weights, back_out, factors, *rest):
    parts, (arrived, back, sems) = rest[:LATE_PARTS], rest[LATE_PARTS:]
    sources, _, width = arrived.shape
    hidden_width = weights.shape[0]
    scale = hidden_width ** (-0.5)
    rows = (sources * CAP, width)
    block = (sources, CAP, width)
    halves = (slice(0, CAP), slice(CAP, 2 * CAP))
    loads = [
        pltpu.make_async_copy(arrived_in.at[:, half], arrived.at[:, half], sems.at[k])
        for k, half in enumerate(halves)
    ]
    for load in loads:
        load.start()
    height = rows[0] // len(parts)
    stores = [
        pltpu.make_async_copy(back.at[:, half], back_out.at[:, half], sems.at[2 + k])
        for k, half in enumerate(halves)
    ] + [
        pltpu.make_async_copy(factors.at[k * height : (k + 1) * height], part, sems.at[4 + k])
        for k, part in enumerate(parts)
    ]
    loads[0].wait()
    inputs = arrived[:, halves[0], :].reshape(rows)
    gate_pre = times(inputs, project[:, :hidden_width])
    up_pre = times(inputs, project[:, hidden_width:])
    sigmoid_value = jax.nn.sigmoid(gate_pre)
    activated = gate_pre * sigmoid_value
    hidden = (activated * up_pre).astype(bf16)
    factors[:, :hidden_width] = hidden
    loads[1].wait()
    routed = arrived[:, halves[1], :].reshape(rows)
    factors[:, hidden_width:] = routed
    for store in stores[2:]:
        store.start()
    back[:, halves[0], :] = (times(hidden, weights[...]) * scale).astype(bf16).reshape(block)
    stores[0].start()
    hidden_grad = times(routed, weights[...], 1, 1) * scale
    slope = sigmoid_value * (1.0 + gate_pre * (1.0 - sigmoid_value))
    gate_grad = (hidden_grad * up_pre * slope).astype(bf16)
    up_grad = (hidden_grad * activated).astype(bf16)
    input_grad = times(gate_grad, project[:, :hidden_width], 1, 1) + times(
        up_grad, project[:, hidden_width:], 1, 1
    )
    back[:, halves[1], :] = input_grad.astype(bf16).reshape(block)
    stores[1].start()
    for store in stores:
        store.wait()


def combine_kernel(came_back, shares, picks, layer_out, token_grad):
    experts = came_back.shape[0]
    rows = (experts * CAP, came_back.shape[2])
    share = shares[...]
    upper = share.astype(bf16)
    lower = (share - upper.astype(f32)).astype(bf16)
    outputs = came_back[:, :CAP, :].reshape(rows)
    layer_out[...] = (times(upper, outputs, 0, 0) + times(lower, outputs, 0, 0)).astype(bf16)
    token_grad[...] = times(picks[...], came_back[:, CAP:, :].reshape(rows), 0, 0).astype(bf16)


def stepped(weights, hidden, routed, hidden_width):
    weight_grad = times(hidden, routed, 0, 0) * (hidden_width ** (-0.5))
    return (weights.astype(f32) - step_size * weight_grad).astype(bf16)


def step_kernel(weights, factors, updated):
    hidden_width = weights.shape[0]
    updated[...] = stepped(
        weights[...], factors[:, :hidden_width], factors[:, hidden_width:], hidden_width
    )


def mix_kernel(first, updated, near, *rest):
    far_weights = rest[:EARLY_PARTS]
    far_factors = rest[EARLY_PARTS : EARLY_PARTS + LATE_PARTS]
    mixed, held_factors = rest[EARLY_PARTS + LATE_PARTS :]

    def put(rows, neighbor):
        mixed[rows, :] = (
            (1.0 - mix_share) * updated[rows, :].astype(f32) + mix_share * neighbor.astype(f32)
        ).astype(bf16)

    @pl.when(first[0] == 1)
    def _():
        height = held_factors.shape[0] // LATE_PARTS
        for k, part in enumerate(far_factors):
            held_factors[k * height : (k + 1) * height, :] = part[...]
        hidden_width = updated.shape[0]
        routed = held_factors[:, hidden_width:]
        height = hidden_width // EARLY_PARTS
        for k, part in enumerate(far_weights):
            rows = slice(k * height, (k + 1) * height)
            put(rows, stepped(part[...], held_factors[:, rows], routed, hidden_width))

    @pl.when(first[0] != 1)
    def _():
        put(slice(None), near[...])


def shape(dims, dtype=bf16):
    return jax.ShapeDtypeStruct(dims, dtype)


GRANT = pltpu.CompilerParams(vmem_limit_bytes=20 << 20)
HBM = pl.BlockSpec(memory_space=pltpu.HBM)
VMEM = pl.BlockSpec(memory_space=pltpu.VMEM)


def pick(ids, gates, tokens, cotangent, experts):
    count, width = tokens.shape
    outs = (
        shape((experts, 2 * CAP, width)),
        shape((experts * CAP, count), f32),
        shape((experts * CAP, count)),
    )
    ins = (ids, gates, tokens, cotangent)
    return pl.pallas_call(
        pick_kernel,
        out_shape=tuple(pltpu.HBM(x.shape, x.dtype) for x in outs),
        in_specs=[HBM] * len(ins),
        out_specs=[HBM] * len(outs),
        scratch_shapes=[pltpu.VMEM(x.shape, x.dtype) for x in ins + outs]
        + [pltpu.SemaphoreType.DMA((8,))],
        compiler_params=GRANT,
        name="pick",
    )(*(pltpu.with_memory_space_constraint(x, pltpu.HBM) for x in ins))


def expert_pass(arrived, project, weights):
    rows = arrived.shape[0] * CAP
    columns = weights.shape[0] + weights.shape[1]
    return pl.pallas_call(
        expert_kernel,
        out_shape=(pltpu.HBM(arrived.shape, bf16), shape((rows, columns)))
        + (pltpu.HBM((rows // LATE_PARTS, columns), bf16),) * LATE_PARTS,
        in_specs=[HBM, VMEM, VMEM],
        out_specs=[HBM, VMEM] + [HBM] * LATE_PARTS,
        scratch_shapes=[
            pltpu.VMEM(arrived.shape, bf16),
            pltpu.VMEM(arrived.shape, bf16),
            pltpu.SemaphoreType.DMA((4 + LATE_PARTS,)),
        ],
        compiler_params=GRANT,
        name="expert_pass",
    )(arrived, project, weights)


def combine(came_back, shares, picks):
    count = shares.shape[1]
    width = came_back.shape[2]
    return pl.pallas_call(
        combine_kernel,
        out_shape=(shape((count, width)), shape((count, width))),
        compiler_params=GRANT,
        name="combine",
    )(came_back, shares, picks)


def step(weights, factors):
    return pl.pallas_call(
        step_kernel, out_shape=shape(weights.shape), compiler_params=GRANT, name="step"
    )(weights, factors)


def mix(first, updated, near, far_weights, far_factors):
    rows, columns = far_factors[0].shape
    return pl.pallas_call(
        mix_kernel,
        out_shape=shape(updated.shape),
        in_specs=[pl.BlockSpec(memory_space=pltpu.SMEM)]
        + [VMEM] * (2 + len(far_weights) + len(far_factors)),
        out_specs=VMEM,
        scratch_shapes=[pltpu.VMEM((rows * LATE_PARTS, columns), bf16)],
        compiler_params=GRANT,
        name="mix",
    )(first, updated, near, *far_weights, *far_factors)


def planes_of():
    return range(0, lax.axis_size("replica"), PLANE)


def to_next(array):
    route = [(h + i, h + i + 1) for h in planes_of() for i in range(PLANE - 1)]
    return lax.ppermute(array, "replica", route)


def to_next_plane(pieces, places):
    held = []
    for piece, between in zip(pieces, places):
        if between == LAST:
            held.append(piece)
            continue
        route = [(h + LAST, h + between) for h in planes_of()]
        held.append(lax.ppermute(piece, "replica", route))
    far = []
    for piece, between in zip(held, places):
        route = [(h + between, (h + PLANE) % lax.axis_size("replica")) for h in planes_of()]
        far.append(lax.ppermute(piece, "replica", route))
    return far


def on_device(tokens, cotangent, expert_ids, gate_weights, gate_up, down_weights):
    experts = lax.axis_size("expert")
    weights = down_weights[0, 0]
    project = gate_up[0]
    sent, shares, picks = pick(expert_ids.T, gate_weights.T, tokens, cotangent, experts)
    arrived = lax.all_to_all(sent, "expert", split_axis=0, concat_axis=0, tiled=True)
    height = weights.shape[0] // EARLY_PARTS
    pieces = [weights[k * height : (k + 1) * height] for k in range(EARLY_PARTS)]
    far_weights = to_next_plane(pieces, EARLY_FROM)
    back, factors, *parts = expert_pass(arrived, project, weights)
    came_back = lax.all_to_all(back, "expert", split_axis=0, concat_axis=0, tiled=True)
    updated = step(weights, factors)
    far_factors = to_next_plane(parts, LATE_FROM)
    near = to_next(updated)
    first = (lax.axis_index("replica") % PLANE == 0).astype(jnp.int32).reshape(1)
    mixed = mix(first, updated, near, far_weights, far_factors)
    layer_out, token_grad = combine(came_back, shares, picks)
    return (layer_out, token_grad, mixed[None, None])


def solution(mesh):
    return jax.shard_map(
        on_device,
        mesh=mesh,
        in_specs=(
            P(("replica", "expert"), None),
            P(("replica", "expert"), None),
            P(("replica", "expert"), None),
            P(("replica", "expert"), None),
            P("expert", None, None),
            P("replica", "expert", None, None),
        ),
        out_specs=(
            P(("replica", "expert"), None),
            P(("replica", "expert"), None),
            P("replica", "expert", None, None),
        ),
        check_vma=False,
    )
```

```python
import jax
import jax.numpy as jnp
from jax import lax
from jax.experimental import pallas as pl
from jax.experimental.pallas import tpu as pltpu
from jax.sharding import PartitionSpec as P

CAP = 16
PLANE = 32


step_size = 2.0
mix_share = 0.5

f32 = jnp.float32
bf16 = jnp.bfloat16


def place(y, x, core):
    return (y * 4 + x) * 2 + core


LAST = place(3, 3, 1)
EARLY_FROM = (
    place(1, 0, 0),
    place(1, 3, 0),
    place(1, 1, 0),
    place(1, 2, 0),
    place(0, 2, 0),
    place(2, 0, 0),
)
EARLY_ROWS = (96, 96, 80, 80, 80, 80)
LATE_FROM = (
    place(3, 0, 0),
    place(0, 3, 0),
    place(0, 0, 1),
    place(3, 2, 0),
    place(2, 3, 0),
    LAST,
)
LATE_ROWS = (32, 32, 16, 16, 16, 16)
BEFORE_FROM = (place(3, 0, 0), LAST)
BEFORE_ROWS = (48, 80)
EARLY_PARTS = len(EARLY_FROM)
BEFORE_PARTS = len(BEFORE_FROM)
LATE_PARTS = len(LATE_FROM)


def times(left, right, left_dim=1, right_dim=0):
    return lax.dot_general(
        left, right, (((left_dim,), (right_dim,)), ((), ())), preferred_element_type=f32
    )


def pick_kernel(ids_in, gates_in, tokens_in, cotangent_in, sent_out, shares_out, picks_out, *own):
    ids, gates, tokens, cotangent, sent, shares, picks, sems = own
    loads = [
        pltpu.make_async_copy(source, target, sems.at[k])
        for k, (source, target) in enumerate(
            ((ids_in, ids), (gates_in, gates), (tokens_in, tokens), (cotangent_in, cotangent))
        )
    ]
    for load in loads:
        load.start()
    experts = sent.shape[0]
    count, width = tokens.shape
    loads[0].wait()
    loads[1].wait()
    all_ids, all_gates = ids[...], gates[...]
    named_rows, share_rows = [], []
    for e in range(experts):
        hits = all_ids == e
        named_rows.append(jnp.max(hits.astype(f32), axis=0, keepdims=True))
        share_rows.append(jnp.sum(jnp.where(hits, all_gates, 0.0), axis=0, keepdims=True))
    named = jnp.concatenate(named_rows, axis=0)
    before = (
        lax.broadcasted_iota(jnp.int32, (count, count), 0)
        <= lax.broadcasted_iota(jnp.int32, (count, count), 1)
    ).astype(bf16)
    position = jnp.where(named > 0.0, times(named.astype(bf16), before), 0.0).astype(jnp.int32)
    slot = lax.broadcasted_iota(jnp.int32, (CAP, count), 0) + 1
    picked = jnp.concatenate(
        [jnp.broadcast_to(position[e : e + 1], (CAP, count)) == slot for e in range(experts)],
        axis=0,
    )
    share = jnp.concatenate(
        [jnp.broadcast_to(share_rows[e], (CAP, count)) for e in range(experts)], axis=0
    )
    share = jnp.where(picked, share, 0.0)
    shares[...] = share
    picked = picked.astype(bf16)
    picks[...] = picked
    rows = (experts, CAP, width)
    first, second = slice(0, CAP), slice(CAP, 2 * CAP)
    stores = [
        pltpu.make_async_copy(shares, shares_out, sems.at[4]),
        pltpu.make_async_copy(picks, picks_out, sems.at[5]),
        pltpu.make_async_copy(sent.at[:, first], sent_out.at[:, first], sems.at[6]),
        pltpu.make_async_copy(sent.at[:, second], sent_out.at[:, second], sems.at[7]),
    ]
    stores[0].start()
    stores[1].start()
    loads[2].wait()
    sent[:, first, :] = times(picked, tokens[...]).astype(bf16).reshape(rows)
    stores[2].start()
    slot_share = jnp.sum(share, axis=1, keepdims=True)
    loads[3].wait()
    sent[:, second, :] = (slot_share * times(picked, cotangent[...])).astype(bf16).reshape(rows)
    stores[3].start()
    for store in stores:
        store.wait()


def expert_kernel(arrived_in, project, weights, back_out, factors, *rest):
    parts, (arrived, back, sems) = rest[:-3], rest[-3:]
    sources, _, width = arrived.shape
    hidden_width = weights.shape[0]
    scale = hidden_width ** (-0.5)
    rows = (sources * CAP, width)
    block = (sources, CAP, width)
    halves = (slice(0, CAP), slice(CAP, 2 * CAP))
    loads = [
        pltpu.make_async_copy(arrived_in.at[:, half], arrived.at[:, half], sems.at[k])
        for k, half in enumerate(halves)
    ]
    for load in loads:
        load.start()
    stores = [
        pltpu.make_async_copy(back.at[:, half], back_out.at[:, half], sems.at[2 + k])
        for k, half in enumerate(halves)
    ]
    row = 0
    for k, part in enumerate(parts):
        height = part.shape[0]
        stores.append(pltpu.make_async_copy(factors.at[row : row + height], part, sems.at[4 + k]))
        row = (row + height) % rows[0]
    loads[0].wait()
    inputs = arrived[:, halves[0], :].reshape(rows)
    gate_pre = times(inputs, project[:, :hidden_width])
    up_pre = times(inputs, project[:, hidden_width:])
    sigmoid_value = jax.nn.sigmoid(gate_pre)
    activated = gate_pre * sigmoid_value
    hidden = (activated * up_pre).astype(bf16)
    factors[:, :hidden_width] = hidden
    loads[1].wait()
    routed = arrived[:, halves[1], :].reshape(rows)
    factors[:, hidden_width:] = routed
    for store in stores[2:]:
        store.start()
    back[:, halves[0], :] = (times(hidden, weights[...]) * scale).astype(bf16).reshape(block)
    stores[0].start()
    hidden_grad = times(routed, weights[...], 1, 1) * scale
    slope = sigmoid_value * (1.0 + gate_pre * (1.0 - sigmoid_value))
    gate_grad = (hidden_grad * up_pre * slope).astype(bf16)
    up_grad = (hidden_grad * activated).astype(bf16)
    input_grad = times(gate_grad, project[:, :hidden_width], 1, 1) + times(
        up_grad, project[:, hidden_width:], 1, 1
    )
    back[:, halves[1], :] = input_grad.astype(bf16).reshape(block)
    stores[1].start()
    for store in stores:
        store.wait()


def combine_kernel(came_back, shares, picks, layer_out, token_grad):
    experts = came_back.shape[0]
    rows = (experts * CAP, came_back.shape[2])
    share = shares[...]
    upper = share.astype(bf16)
    lower = (share - upper.astype(f32)).astype(bf16)
    outputs = came_back[:, :CAP, :].reshape(rows)
    layer_out[...] = (times(upper, outputs, 0, 0) + times(lower, outputs, 0, 0)).astype(bf16)
    token_grad[...] = times(picks[...], came_back[:, CAP:, :].reshape(rows), 0, 0).astype(bf16)


def stepped(weights, hidden, routed, hidden_width):
    weight_grad = times(hidden, routed, 0, 0) * (hidden_width ** (-0.5))
    return (weights.astype(f32) - step_size * weight_grad).astype(bf16)


def step_kernel(weights, factors, updated):
    hidden_width = weights.shape[0]
    updated[...] = stepped(
        weights[...], factors[:, :hidden_width], factors[:, hidden_width:], hidden_width
    )


def mix_kernel(first, updated, near, *rest):
    far_weights = rest[:EARLY_PARTS]
    far_after = rest[EARLY_PARTS : EARLY_PARTS + LATE_PARTS]
    far_before = rest[EARLY_PARTS + LATE_PARTS : -3]
    mixed, held_weights, held_factors = rest[-3:]

    def put(neighbor):
        mixed[...] = (
            (1.0 - mix_share) * updated[...].astype(f32) + mix_share * neighbor.astype(f32)
        ).astype(bf16)

    def hold(held, parts):
        row = 0
        for part in parts:
            held[row : row + part.shape[0], :] = part[...]
            row += part.shape[0]

    @pl.when(first[0] == 1)
    def _():
        hold(held_factors, far_after)

    @pl.when(first[0] == 2)
    def _():
        hold(held_factors, far_before)

    @pl.when(first[0] != 0)
    def _():
        hold(held_weights, far_weights)
        hidden_width = updated.shape[0]
        hidden, routed = held_factors[:, :hidden_width], held_factors[:, hidden_width:]
        put(stepped(held_weights[...], hidden, routed, hidden_width))

    @pl.when(first[0] == 0)
    def _():
        put(near[...])


def shape(dims, dtype=bf16):
    return jax.ShapeDtypeStruct(dims, dtype)


GRANT = pltpu.CompilerParams(vmem_limit_bytes=20 << 20)
HBM = pl.BlockSpec(memory_space=pltpu.HBM)
VMEM = pl.BlockSpec(memory_space=pltpu.VMEM)


def pick(ids, gates, tokens, cotangent, experts):
    count, width = tokens.shape
    outs = (
        shape((experts, 2 * CAP, width)),
        shape((experts * CAP, count), f32),
        shape((experts * CAP, count)),
    )
    ins = (ids, gates, tokens, cotangent)
    return pl.pallas_call(
        pick_kernel,
        out_shape=tuple(pltpu.HBM(x.shape, x.dtype) for x in outs),
        in_specs=[HBM] * len(ins),
        out_specs=[HBM] * len(outs),
        scratch_shapes=[pltpu.VMEM(x.shape, x.dtype) for x in ins + outs]
        + [pltpu.SemaphoreType.DMA((8,))],
        compiler_params=GRANT,
        name="pick",
    )(*(pltpu.with_memory_space_constraint(x, pltpu.HBM) for x in ins))


def expert_pass(arrived, project, weights):
    rows = arrived.shape[0] * CAP
    columns = weights.shape[0] + weights.shape[1]
    return pl.pallas_call(
        expert_kernel,
        out_shape=(pltpu.HBM(arrived.shape, bf16), shape((rows, columns)))
        + tuple(pltpu.HBM((height, columns), bf16) for height in BEFORE_ROWS + LATE_ROWS),
        in_specs=[HBM, VMEM, VMEM],
        out_specs=[HBM, VMEM] + [HBM] * (BEFORE_PARTS + LATE_PARTS),
        scratch_shapes=[
            pltpu.VMEM(arrived.shape, bf16),
            pltpu.VMEM(arrived.shape, bf16),
            pltpu.SemaphoreType.DMA((4 + BEFORE_PARTS + LATE_PARTS,)),
        ],
        compiler_params=GRANT,
        name="expert_pass",
    )(arrived, project, weights)


def combine(came_back, shares, picks):
    count = shares.shape[1]
    width = came_back.shape[2]
    return pl.pallas_call(
        combine_kernel,
        out_shape=(shape((count, width)), shape((count, width))),
        compiler_params=GRANT,
        name="combine",
    )(came_back, shares, picks)


def step(weights, factors):
    return pl.pallas_call(
        step_kernel, out_shape=shape(weights.shape), compiler_params=GRANT, name="step"
    )(weights, factors)


def mix(first, updated, near, far_weights, far_after, far_before):
    rows = sum(LATE_ROWS)
    columns = far_after[0].shape[1]
    far = (*far_weights, *far_after, *far_before)
    return pl.pallas_call(
        mix_kernel,
        out_shape=shape(updated.shape),
        in_specs=[pl.BlockSpec(memory_space=pltpu.SMEM)]
        + [VMEM] * (2 + len(far)),
        out_specs=VMEM,
        scratch_shapes=[
            pltpu.VMEM(updated.shape, bf16),
            pltpu.VMEM((rows, columns), bf16),
        ],
        compiler_params=GRANT,
        name="mix",
    )(first, updated, near, *far)


def planes_of():
    return range(0, lax.axis_size("replica"), PLANE)


def to_next(array):
    route = [(h + i, h + i + 1) for h in planes_of() for i in range(PLANE - 1)]
    return lax.ppermute(array, "replica", route)


def to_next_plane(pieces, places, planes):
    held = []
    for piece, between in zip(pieces, places):
        if between == LAST:
            held.append(piece)
            continue
        route = [(h + LAST, h + between) for h in planes]
        held.append(lax.ppermute(piece, "replica", route))
    far = []
    for piece, between in zip(held, places):
        route = [(h + between, (h + PLANE) % lax.axis_size("replica")) for h in planes]
        far.append(lax.ppermute(piece, "replica", route))
    return far


def on_device(tokens, cotangent, expert_ids, gate_weights, gate_up, down_weights):
    experts = lax.axis_size("expert")
    weights = down_weights[0, 0]
    project = gate_up[0]
    sent, shares, picks = pick(expert_ids.T, gate_weights.T, tokens, cotangent, experts)
    arrived = lax.all_to_all(sent, "expert", split_axis=0, concat_axis=0, tiled=True)
    pieces, row = [], 0
    for height in EARLY_ROWS:
        pieces.append(weights[row : row + height])
        row += height
    far_weights = to_next_plane(pieces, EARLY_FROM, planes_of())
    back, factors, *parts = expert_pass(arrived, project, weights)
    came_back = lax.all_to_all(back, "expert", split_axis=0, concat_axis=0, tiled=True)
    updated = step(weights, factors)
    planes = planes_of()
    far_before = to_next_plane(parts[:BEFORE_PARTS], BEFORE_FROM, planes[-1:])
    far_after = to_next_plane(parts[BEFORE_PARTS:], LATE_FROM, planes[:-1])
    near = to_next(updated)
    place_index = lax.axis_index("replica")
    first = jnp.where(place_index % PLANE == 0, jnp.where(place_index == 0, 2, 1), 0)
    first = first.astype(jnp.int32).reshape(1)
    mixed = mix(first, updated, near, far_weights, far_after, far_before)
    layer_out, token_grad = combine(came_back, shares, picks)
    return (layer_out, token_grad, mixed[None, None])


def solution(mesh):
    return jax.shard_map(
        on_device,
        mesh=mesh,
        in_specs=(
            P(("replica", "expert"), None),
            P(("replica", "expert"), None),
            P(("replica", "expert"), None),
            P(("replica", "expert"), None),
            P("expert", None, None),
            P("replica", "expert", None, None),
        ),
        out_specs=(
            P(("replica", "expert"), None),
            P(("replica", "expert"), None),
            P("replica", "expert", None, None),
        ),
        check_vma=False,
    )
```

```python
import jax
import jax.numpy as jnp
from jax import lax
from jax.experimental import pallas as pl
from jax.experimental.pallas import tpu as pltpu
from jax.sharding import PartitionSpec as P

CAP = 16
PLANE = 32


step_size = 2.0
mix_share = 0.5

f32 = jnp.float32
bf16 = jnp.bfloat16


def place(y, x, core):
    return (y * 4 + x) * 2 + core


LAST = place(3, 3, 1)
EARLY_FROM = (
    place(1, 0, 0),
    place(1, 3, 0),
    place(1, 1, 0),
    place(1, 2, 0),
    place(0, 2, 0),
    place(2, 0, 0),
)
EARLY_ROWS = (96, 96, 80, 80, 80, 80)
LATE_FROM = (
    place(3, 0, 0),
    place(0, 3, 0),
    place(0, 0, 1),
    place(3, 2, 0),
    LAST,
)
LATE_ROWS = (32, 32, 32, 16, 16)
BEFORE_FROM = (place(3, 0, 0), LAST)
BEFORE_ROWS = (48, 80)
EARLY_PARTS = len(EARLY_FROM)
BEFORE_PARTS = len(BEFORE_FROM)
LATE_PARTS = len(LATE_FROM)


def times(left, right, left_dim=1, right_dim=0):
    return lax.dot_general(
        left, right, (((left_dim,), (right_dim,)), ((), ())), preferred_element_type=f32
    )


def pick_kernel(ids_in, gates_in, tokens_in, cotangent_in, sent_out, shares_out, *own):
    ids, gates, tokens, cotangent, sent, shares, sems = own
    loads = [
        pltpu.make_async_copy(source, target, sems.at[k])
        for k, (source, target) in enumerate(
            ((ids_in, ids), (gates_in, gates), (tokens_in, tokens), (cotangent_in, cotangent))
        )
    ]
    for load in loads:
        load.start()
    experts = sent.shape[0]
    count, width = tokens.shape
    loads[0].wait()
    loads[1].wait()
    all_ids, all_gates = ids[...], gates[...]
    named_rows, share_rows = [], []
    for e in range(experts):
        hits = all_ids == e
        named_rows.append(jnp.max(hits.astype(f32), axis=0, keepdims=True))
        share_rows.append(jnp.sum(jnp.where(hits, all_gates, 0.0), axis=0, keepdims=True))
    named = jnp.concatenate(named_rows, axis=0)
    before = (
        lax.broadcasted_iota(jnp.int32, (count, count), 0)
        <= lax.broadcasted_iota(jnp.int32, (count, count), 1)
    ).astype(bf16)
    position = jnp.where(named > 0.0, times(named.astype(bf16), before), 0.0).astype(jnp.int32)
    slot = lax.broadcasted_iota(jnp.int32, (CAP, count), 0) + 1
    picked = jnp.concatenate(
        [jnp.broadcast_to(position[e : e + 1], (CAP, count)) == slot for e in range(experts)],
        axis=0,
    )
    share = jnp.concatenate(
        [jnp.broadcast_to(share_rows[e], (CAP, count)) for e in range(experts)], axis=0
    )
    share = jnp.where(picked, share, 0.0)
    shares[...] = share
    picked = picked.astype(bf16)
    rows = (experts, CAP, width)
    first, second = slice(0, CAP), slice(CAP, 2 * CAP)
    stores = [
        pltpu.make_async_copy(shares, shares_out, sems.at[4]),
        pltpu.make_async_copy(sent.at[:, first], sent_out.at[:, first], sems.at[5]),
        pltpu.make_async_copy(sent.at[:, second], sent_out.at[:, second], sems.at[6]),
    ]
    stores[0].start()
    loads[2].wait()
    sent[:, first, :] = times(picked, tokens[...]).astype(bf16).reshape(rows)
    stores[1].start()
    slot_share = jnp.sum(share, axis=1, keepdims=True)
    loads[3].wait()
    sent[:, second, :] = (slot_share * times(picked, cotangent[...])).astype(bf16).reshape(rows)
    stores[2].start()
    for store in stores:
        store.wait()


def expert_kernel(arrived_in, project, weights, back_out, factors, *rest):
    parts, (arrived, back, sems) = rest[:-3], rest[-3:]
    sources, _, width = arrived.shape
    hidden_width = weights.shape[0]
    scale = hidden_width ** (-0.5)
    rows = (sources * CAP, width)
    block = (sources, CAP, width)
    halves = (slice(0, CAP), slice(CAP, 2 * CAP))
    loads = [
        pltpu.make_async_copy(arrived_in.at[:, half], arrived.at[:, half], sems.at[k])
        for k, half in enumerate(halves)
    ]
    for load in loads:
        load.start()
    stores = [
        pltpu.make_async_copy(back.at[:, half], back_out.at[:, half], sems.at[2 + k])
        for k, half in enumerate(halves)
    ]
    row = 0
    for k, part in enumerate(parts):
        height = part.shape[0]
        stores.append(pltpu.make_async_copy(factors.at[row : row + height], part, sems.at[4 + k]))
        row = (row + height) % rows[0]
    loads[0].wait()
    inputs = arrived[:, halves[0], :].reshape(rows)
    gate_pre = times(inputs, project[:, :hidden_width])
    up_pre = times(inputs, project[:, hidden_width:])
    sigmoid_value = jax.nn.sigmoid(gate_pre)
    activated = gate_pre * sigmoid_value
    hidden = (activated * up_pre).astype(bf16)
    factors[:, :hidden_width] = hidden
    loads[1].wait()
    routed = arrived[:, halves[1], :].reshape(rows)
    factors[:, hidden_width:] = routed
    for store in stores[2:]:
        store.start()
    back[:, halves[0], :] = (times(hidden, weights[...]) * scale).astype(bf16).reshape(block)
    stores[0].start()
    hidden_grad = times(routed, weights[...], 1, 1) * scale
    slope = sigmoid_value * (1.0 + gate_pre * (1.0 - sigmoid_value))
    gate_grad = (hidden_grad * up_pre * slope).astype(bf16)
    up_grad = (hidden_grad * activated).astype(bf16)
    input_grad = times(gate_grad, project[:, :hidden_width], 1, 1) + times(
        up_grad, project[:, hidden_width:], 1, 1
    )
    back[:, halves[1], :] = input_grad.astype(bf16).reshape(block)
    stores[1].start()
    for store in stores:
        store.wait()


def combine_kernel(came_back, shares, layer_out, token_grad):
    experts = came_back.shape[0]
    rows = (experts * CAP, came_back.shape[2])
    share = shares[...]
    picks = (share > 0.0).astype(bf16)
    upper = share.astype(bf16)
    lower = (share - upper.astype(f32)).astype(bf16)
    outputs = came_back[:, :CAP, :].reshape(rows)
    layer_out[...] = (times(upper, outputs, 0, 0) + times(lower, outputs, 0, 0)).astype(bf16)
    token_grad[...] = times(picks, came_back[:, CAP:, :].reshape(rows), 0, 0).astype(bf16)


def stepped(weights, hidden, routed, hidden_width):
    weight_grad = times(hidden, routed, 0, 0) * (hidden_width ** (-0.5))
    return (weights.astype(f32) - step_size * weight_grad).astype(bf16)


def step_kernel(weights, factors, updated):
    hidden_width = weights.shape[0]
    updated[...] = stepped(
        weights[...], factors[:, :hidden_width], factors[:, hidden_width:], hidden_width
    )


def mix_kernel(first, updated, near, *rest):
    far_weights = rest[:EARLY_PARTS]
    far_after = rest[EARLY_PARTS : EARLY_PARTS + LATE_PARTS]
    far_before = rest[EARLY_PARTS + LATE_PARTS : -3]
    mixed, held_weights, held_factors = rest[-3:]

    def put(neighbor):
        mixed[...] = (
            (1.0 - mix_share) * updated[...].astype(f32) + mix_share * neighbor.astype(f32)
        ).astype(bf16)

    def hold(held, parts):
        row = 0
        for part in parts:
            held[row : row + part.shape[0], :] = part[...]
            row += part.shape[0]

    @pl.when(first[0] == 1)
    def _():
        hold(held_factors, far_after)

    @pl.when(first[0] == 2)
    def _():
        hold(held_factors, far_before)

    @pl.when(first[0] != 0)
    def _():
        hold(held_weights, far_weights)
        hidden_width = updated.shape[0]
        hidden, routed = held_factors[:, :hidden_width], held_factors[:, hidden_width:]
        put(stepped(held_weights[...], hidden, routed, hidden_width))

    @pl.when(first[0] == 0)
    def _():
        put(near[...])


def shape(dims, dtype=bf16):
    return jax.ShapeDtypeStruct(dims, dtype)


GRANT = pltpu.CompilerParams(vmem_limit_bytes=20 << 20)
HBM = pl.BlockSpec(memory_space=pltpu.HBM)
VMEM = pl.BlockSpec(memory_space=pltpu.VMEM)


def pick(ids, gates, tokens, cotangent, experts):
    count, width = tokens.shape
    outs = (
        shape((experts, 2 * CAP, width)),
        shape((experts * CAP, count), f32),
    )
    ins = (ids, gates, tokens, cotangent)
    return pl.pallas_call(
        pick_kernel,
        out_shape=tuple(pltpu.HBM(x.shape, x.dtype) for x in outs),
        in_specs=[HBM] * len(ins),
        out_specs=[HBM] * len(outs),
        scratch_shapes=[pltpu.VMEM(x.shape, x.dtype) for x in ins + outs]
        + [pltpu.SemaphoreType.DMA((7,))],
        compiler_params=GRANT,
        name="pick",
    )(*(pltpu.with_memory_space_constraint(x, pltpu.HBM) for x in ins))


def expert_pass(arrived, project, weights):
    rows = arrived.shape[0] * CAP
    columns = weights.shape[0] + weights.shape[1]
    return pl.pallas_call(
        expert_kernel,
        out_shape=(pltpu.HBM(arrived.shape, bf16), shape((rows, columns)))
        + tuple(pltpu.HBM((height, columns), bf16) for height in BEFORE_ROWS + LATE_ROWS),
        in_specs=[HBM, VMEM, VMEM],
        out_specs=[HBM, VMEM] + [HBM] * (BEFORE_PARTS + LATE_PARTS),
        scratch_shapes=[
            pltpu.VMEM(arrived.shape, bf16),
            pltpu.VMEM(arrived.shape, bf16),
            pltpu.SemaphoreType.DMA((4 + BEFORE_PARTS + LATE_PARTS,)),
        ],
        compiler_params=GRANT,
        name="expert_pass",
    )(arrived, project, weights)


def combine(came_back, shares):
    count = shares.shape[1]
    width = came_back.shape[2]
    return pl.pallas_call(
        combine_kernel,
        out_shape=(shape((count, width)), shape((count, width))),
        compiler_params=GRANT,
        name="combine",
    )(came_back, shares)


def step(weights, factors):
    return pl.pallas_call(
        step_kernel, out_shape=shape(weights.shape), compiler_params=GRANT, name="step"
    )(weights, factors)


def mix(first, updated, near, far_weights, far_after, far_before):
    rows = sum(LATE_ROWS)
    columns = far_after[0].shape[1]
    far = (*far_weights, *far_after, *far_before)
    return pl.pallas_call(
        mix_kernel,
        out_shape=shape(updated.shape),
        in_specs=[pl.BlockSpec(memory_space=pltpu.SMEM)]
        + [VMEM] * (2 + len(far)),
        out_specs=VMEM,
        scratch_shapes=[
            pltpu.VMEM(updated.shape, bf16),
            pltpu.VMEM((rows, columns), bf16),
        ],
        compiler_params=GRANT,
        name="mix",
    )(first, updated, near, *far)


def planes_of():
    return range(0, lax.axis_size("replica"), PLANE)


def to_next(array):
    route = [(h + i, h + i + 1) for h in planes_of() for i in range(PLANE - 1)]
    return lax.ppermute(array, "replica", route)


def to_next_plane(pieces, places, planes):
    held = []
    for piece, between in zip(pieces, places):
        if between == LAST:
            held.append(piece)
            continue
        route = [(h + LAST, h + between) for h in planes]
        held.append(lax.ppermute(piece, "replica", route))
    far = []
    for piece, between in zip(held, places):
        route = [(h + between, (h + PLANE) % lax.axis_size("replica")) for h in planes]
        far.append(lax.ppermute(piece, "replica", route))
    return far


def on_device(tokens, cotangent, expert_ids, gate_weights, gate_up, down_weights):
    experts = lax.axis_size("expert")
    weights = down_weights[0, 0]
    project = gate_up[0]
    sent, shares = pick(expert_ids.T, gate_weights.T, tokens, cotangent, experts)
    arrived = lax.all_to_all(sent, "expert", split_axis=0, concat_axis=0, tiled=True)
    pieces, row = [], 0
    for height in EARLY_ROWS:
        pieces.append(weights[row : row + height])
        row += height
    far_weights = to_next_plane(pieces, EARLY_FROM, planes_of())
    back, factors, *parts = expert_pass(arrived, project, weights)
    came_back = lax.all_to_all(back, "expert", split_axis=0, concat_axis=0, tiled=True)
    updated = step(weights, factors)
    planes = planes_of()
    far_before = to_next_plane(parts[:BEFORE_PARTS], BEFORE_FROM, planes[-1:])
    far_after = to_next_plane(parts[BEFORE_PARTS:], LATE_FROM, planes[:-1])
    near = to_next(updated)
    place_index = lax.axis_index("replica")
    first = jnp.where(place_index % PLANE == 0, jnp.where(place_index == 0, 2, 1), 0)
    first = first.astype(jnp.int32).reshape(1)
    mixed = mix(first, updated, near, far_weights, far_after, far_before)
    layer_out, token_grad = combine(came_back, shares)
    return (layer_out, token_grad, mixed[None, None])


def solution(mesh):
    return jax.shard_map(
        on_device,
        mesh=mesh,
        in_specs=(
            P(("replica", "expert"), None),
            P(("replica", "expert"), None),
            P(("replica", "expert"), None),
            P(("replica", "expert"), None),
            P("expert", None, None),
            P("replica", "expert", None, None),
        ),
        out_specs=(
            P(("replica", "expert"), None),
            P(("replica", "expert"), None),
            P("replica", "expert", None, None),
        ),
        check_vma=False,
    )
```
